32 devices in a mesh: grp: 2 (over y), ka: 4 (over z), vib: 2 (over core), fin: 2 (over x).
Axes of the slice: x: 2, y: 2, z: 4, core: 2. Of those that a mesh axis runs over, the one named last changes fastest.
Arguments:
- moments: bfloat16 [2, 2048, 2048], P(None, 'vib'), may hold values from -0.125 to 0.125
- initial_vectors: bfloat16 [8, 2048, 2048], P('ka', 'vib', 'grp'), parts along dimension 2, may hold values from -6 to 6
- final_vectors: bfloat16 [8, 2048, 1024], P('ka', 'vib', ('grp', 'fin')), parts along dimension 2, may hold values from -0.046875 to 0.046875
- basis_counts: int32 [16], P(('grp', 'ka')), parts along dimension 0, may hold values from 512 to 2048
Outputs:
- strengths: float32 [2048, 512], P(('grp', 'ka', 'vib'), 'fin'), parts along dimension 0
The draws below stay inside these ranges and needn't reach their ends.
There are 2 independent parts, one for each index of `grp`. The reference program is written for one: setup_inputs(seed, part) draws one part's arguments, and reference() takes and returns one part's arrays. A program takes and returns all parts, laid end to end along the dimension named above; an argument that names none is the same for every part. Nothing has to cross between parts.
All inputs are finite; a program needn't handle non-finite values.
Results may differ from the reference program's by a relative error of at most 0.0003.
Values may be sent and summed in bfloat16 or wider, within the bound.
No kernel may reach another device: no remote copies, remote signals or barrier semaphores. Data moves between devices by JAX's collectives and lax.ppermute only.
A program may use at most 64 MiB of HBM per device.

```python
import jax
import jax.numpy as jnp
from jax import lax

NV = 2048
NI = 1024
NF = 512
JQ = 30
KB = 8


def place_ends(entries, rng, least, largest):
    extent = entries.shape
    spot = [jax.random.randint(jax.random.fold_in(rng, axis), (), 0, extent[axis]) for axis in range(len(extent))]
    entries = entries.at[tuple(spot)].set(least)
    longest = extent.index(max(extent))
    spot[longest] = (spot[longest] + 1) % extent[longest]
    return entries.at[tuple(spot)].set(largest)


def block_scale(stream_key, extent, shards, smallest, top_value):
    def one(axis_at, shards_of):
        steps = jax.random.uniform(jax.random.fold_in(jax.random.fold_in(stream_key, 6), axis_at), (shards_of,), jnp.float32, smallest / len(shards), top_value / len(shards))
        return jnp.repeat(jnp.exp(steps), extent[axis_at] // shards_of).reshape((-1,) + (1,) * (len(extent) - axis_at - 1))

    loudness = one(*shards[0])
    for cut in shards[1:]:
        loudness = loudness * one(*cut)
    return loudness


def gaussian(key, shape, deviation, limit, shards=(), held_as=jnp.bfloat16):
    drawn = jax.random.normal(key, shape, jnp.float32) * deviation
    if len(shards) > 0:
        drawn = block_scale(key, shape, shards, -0.22, 0.18) * drawn
    return jnp.clip(drawn, min=-limit, max=limit).astype(held_as)


def setup_inputs(seed: int = 0, part: int = 0) -> dict:
    streams_of = jax.random.split(jax.random.key(seed), 5)
    own_keys = jax.random.split(jax.random.fold_in(streams_of[4], part), 5)
    return {
        "moments": gaussian(streams_of[0], (2, NV, NV), NV ** -0.5, 0.125, ((1, 2),)),
        "initial_vectors": gaussian(own_keys[1], (KB, NV, NI), 1.0, 6.0, ((0, 4), (1, 2))),
        "final_vectors": gaussian(own_keys[2], (KB, NV, NF), (NV * KB) ** -0.5, 0.046875, ((0, 4), (1, 2), (2, 2))),
        "basis_counts": place_ends(jax.random.randint(own_keys[3], (KB,), NV // 4, NV + 1), jax.random.fold_in(own_keys[3], 1), NV // 4, NV).astype(jnp.int32),
    }


def reference(moments, initial_vectors, final_vectors, basis_counts):
    row_index = jnp.arange(NV, dtype=jnp.int32)
    keep_mask = row_index[None, :] < basis_counts[:, None]
    initial_live = jnp.where(keep_mask[:, :, None], initial_vectors, jnp.zeros((), initial_vectors.dtype))
    final_live = jnp.where(keep_mask[:, :, None], final_vectors, jnp.zeros((), final_vectors.dtype))
    moment_f32 = moments.astype(jnp.float32)

    def project_block(eigen_block):
        return jnp.einsum('cvw,vi->cwi', moment_f32, eigen_block.astype(jnp.float32), precision=lax.Precision.HIGHEST)
    projected = lax.map(project_block, initial_live)
    jsquare = float(JQ * (JQ + 1))
    norm_j = jnp.sqrt(jnp.float32(jsquare))
    k_value = (jnp.arange(KB, dtype=jnp.int32) - KB // 2).astype(jnp.float32)
    coef_same = k_value / norm_j
    coef_upper = 0.5 * jnp.sqrt(jsquare - k_value * (k_value + 1.0)) / norm_j
    coef_lower = -0.5 * jnp.sqrt(jsquare - k_value * (k_value - 1.0)) / norm_j
    along_z = projected[:, 0]
    along_x = projected[:, 1]
    zero_block = jnp.zeros_like(along_x[:1])
    upper_x = jnp.concatenate([along_x[1:], zero_block], axis=0)
    lower_x = jnp.concatenate([zero_block, along_x[:-1]], axis=0)
    coupled = coef_same[:, None, None] * along_z + coef_upper[:, None, None] * upper_x + coef_lower[:, None, None] * lower_x
    amplitude = jnp.einsum('kvf,kvi->if', final_live.astype(jnp.float32), coupled, precision=lax.Precision.HIGHEST)
    return amplitude * amplitude
```

```python
import functools

import jax
import jax.numpy as jnp
import numpy as np
from jax import lax
from jax.experimental import pallas as pl
from jax.experimental.pallas import tpu as pltpu
from jax.sharding import PartitionSpec as P

JQ = 30
CHUNKS = 1
BF16, F32 = jnp.bfloat16, jnp.float32


def coefficient_table(positions, kblocks):
    total = positions * kblocks
    jsquare = np.float32(JQ * (JQ + 1))
    norm = np.sqrt(jsquare)
    k = (np.arange(total) - total // 2).astype(np.float32)
    same = k / norm
    upper = np.float32(0.5) * np.sqrt(jsquare - k * (k + np.float32(1.0))) / norm
    lower = np.float32(-0.5) * np.sqrt(jsquare - k * (k - np.float32(1.0))) / norm
    rows = []
    for a in range(positions):
        first, last = a * kblocks, a * kblocks + 1
        before = upper[first - 1] if first > 0 else 0.0
        after = lower[last + 1] if last + 1 < total else 0.0
        rows.append([same[first], same[last], lower[last], upper[first], before, after, 0.0, 0.0])
    return np.asarray(rows, np.float32)


def mask_rows(x, count, start):
    row = lax.broadcasted_iota(jnp.int32, x.shape, 0) + start
    return jnp.where(row < count, x.astype(F32), 0.0).astype(x.dtype)


def pack_kernel(chunks, place, counts, final, *outs):
    parity, core = place[0], place[1]
    rows, width = final.shape[1], final.shape[2] // chunks
    for slot in range(2):
        k = 1 - parity if slot == 0 else parity
        block = mask_rows(final[k], counts[k], core * rows)
        for c in range(chunks):
            outs[2 * c + slot][...] = block[:, c * width : (c + 1) * width]


def own_kernel(chunks, place, counts, coefs, moments, mine, other, *rest):
    outs, rhs = rest[:chunks], rest[chunks]
    core = place[1]
    kblocks, rows, states = mine.shape
    width = states // chunks

    @pl.when(pl.program_id(0) == 0)
    def _():
        for half, source in ((core, mine), (1 - core, other)):
            start = pl.multiple_of(half * rows, rows)
            for k in range(kblocks):
                block = mask_rows(source[k], counts[k], start)
                for c in range(chunks):
                    at = (c * kblocks + k) * width
                    rhs[pl.ds(start, rows), at : at + width] = block[:, c * width : (c + 1) * width]

    z = jnp.dot(moments[0], rhs[...], preferred_element_type=F32)
    x = jnp.dot(moments[1], rhs[...], preferred_element_type=F32)
    for c in range(chunks):
        lo, mid, hi = (2 * c) * width, (2 * c + 1) * width, (2 * c + 2) * width
        outs[c][:, :width] = coefs[0] * z[:, lo:mid] + coefs[2] * x[:, mid:hi]
        outs[c][:, width:] = coefs[1] * z[:, mid:hi] + coefs[3] * x[:, lo:mid]


def transpose_kernel(x, out):
    out[...] = x[0].T


def halo_kernel(
    places, place, counts, coefs, moments, pair_mine, pair_other, next_mine, next_other,
    partial, init_low, init_high, to_other, to_own, rhs, total,
):
    parity, core, position = place[0], place[1], place[2]
    rows, width = pair_mine.shape
    step, steps = pl.program_id(0), pl.num_programs(0)

    @pl.when(step == 0)
    def _():
        pair_at = pl.multiple_of((1 - parity) * width, width)
        next_at = pl.multiple_of(parity * width, width)
        mine_at = pl.multiple_of(core * rows, rows)
        other_at = pl.multiple_of((1 - core) * rows, rows)
        rhs[pl.ds(mine_at, rows), pl.ds(pair_at, width)] = pair_mine[...]
        rhs[pl.ds(other_at, rows), pl.ds(pair_at, width)] = pair_other[...]
        rhs[pl.ds(mine_at, rows), pl.ds(next_at, width)] = next_mine[...]
        rhs[pl.ds(other_at, rows), pl.ds(next_at, width)] = next_other[...]
        total[...] = jnp.zeros_like(total)

    x = jnp.dot(moments[0], rhs[...], preferred_element_type=F32)
    block = x.shape[0]
    row = lax.broadcasted_iota(jnp.int32, (block, width), 0) + core * rows + step * block
    for k, init in ((0, init_low), (1, init_high)):
        cols = slice(k * width, (k + 1) * width)
        image = partial[:, cols] + coefs[4 + k] * x[:, cols]
        image = jnp.where(row < counts[k], image, 0.0)
        high = image.astype(BF16)
        low = (image - high.astype(F32)).astype(BF16)
        both = jnp.dot(init[...], jnp.concatenate([high, low], axis=1), preferred_element_type=F32)
        total[...] += both[:, :width] + both[:, width:]

    @pl.when(step == steps - 1)
    def _():
        share = to_own.shape[0] // places
        for s in range(places):
            dest = lax.rem(position + s, places)
            own_at = pl.multiple_of((dest * 2 + core) * share, share)
            other_at = pl.multiple_of((dest * 2 + 1 - core) * share, share)
            to_own[s * share : (s + 1) * share, :] = total[pl.ds(own_at, share), :]
            to_other[s * share : (s + 1) * share, :] = total[pl.ds(other_at, share), :]


def add_kernel(mine, other, *outs):
    share = outs[0].shape[0]
    for s, out in enumerate(outs):
        rows = slice(s * share, (s + 1) * share)
        out[...] = mine[rows, :] + other[rows, :]


def finish_kernel(places, *refs):
    out = refs[-1]
    width = refs[0].shape[1]
    for c in range((len(refs) - 1) // places):
        terms = refs[c * places : (c + 1) * places]
        amplitude = terms[0][...]
        for term in terms[1:]:
            amplitude = amplitude + term[...]
        out[:, c * width : (c + 1) * width] = amplitude * amplitude


def cost(flops, moved):
    return pl.CostEstimate(flops=int(flops), bytes_accessed=int(moved), transcendentals=0)


def on_device(moments, initial_vectors, final_vectors, basis_counts):
    kblocks, rows, states = initial_vectors.shape
    finals = final_vectors.shape[2]
    whole = moments.shape[2]
    places, cores = lax.axis_size("ka"), lax.axis_size("vib")
    if kblocks != 2 or cores != 2 or places % 2:
        raise ValueError("unsupported mesh")
    chunks = CHUNKS if finals % (CHUNKS * 128) == 0 else 1
    width = finals // chunks
    share = states // (places * cores)

    position, core = lax.axis_index("ka"), lax.axis_index("vib")
    table = np.asarray(
        [[a % 2, b, a, 0] for a in range(places) for b in range(cores)], np.int32
    )
    place = lax.dynamic_index_in_dim(jnp.asarray(table), position * cores + core, 0, False)
    coefs = lax.dynamic_index_in_dim(
        jnp.asarray(coefficient_table(places, kblocks)), position, 0, False
    )

    swap = [(0, 1), (1, 0)]
    pair = [(a, a + 1 - 2 * (a % 2)) for a in range(places)]
    other_side = [(a, min(max(a - 1 + 2 * (a % 2), 0), places - 1)) for a in range(places)]
    smem = pl.BlockSpec(memory_space=pltpu.SMEM)
    vmem = pl.BlockSpec(memory_space=pltpu.VMEM)

    final_other = lax.ppermute(final_vectors, "vib", swap)

    payload = pl.pallas_call(
        functools.partial(pack_kernel, chunks),
        out_shape=[jax.ShapeDtypeStruct((rows, width), BF16)] * (2 * chunks),
        in_specs=[smem, smem, vmem],
        out_specs=[vmem] * (2 * chunks),
        cost_estimate=cost(0, 4 * kblocks * rows * finals),
        name="pack",
    )(place, basis_counts, final_vectors)
    halo = []
    for c in range(chunks):
        near = lax.ppermute(payload[2 * c], "ka", pair)
        far = lax.ppermute(payload[2 * c + 1], "ka", other_side)
        halo.append((near, far))

    tile = 256
    init_t = pl.pallas_call(
        transpose_kernel,
        out_shape=jax.ShapeDtypeStruct((states, kblocks * rows), BF16),
        grid=(kblocks, rows // tile),
        in_specs=[pl.BlockSpec((1, tile, states), lambda k, j: (k, j, 0))],
        out_specs=pl.BlockSpec((states, tile), lambda k, j: (0, k * (rows // tile) + j)),
        cost_estimate=cost(0, 4 * kblocks * rows * states),
        name="turn",
    )(initial_vectors)

    block = 256
    partial = pl.pallas_call(
        functools.partial(own_kernel, chunks),
        out_shape=[jax.ShapeDtypeStruct((rows, kblocks * width), F32)] * chunks,
        grid=(rows // block,),
        in_specs=[
            smem,
            smem,
            smem,
            pl.BlockSpec((2, block, whole), lambda j: (0, j, 0)),
            pl.BlockSpec((kblocks, rows, finals), lambda j: (0, 0, 0)),
            pl.BlockSpec((kblocks, rows, finals), lambda j: (0, 0, 0)),
        ],
        out_specs=[pl.BlockSpec((block, kblocks * width), lambda j: (j, 0))] * chunks,
        scratch_shapes=[pltpu.VMEM((whole, kblocks * finals), BF16)],
        cost_estimate=cost(
            4 * rows * whole * kblocks * finals, 2 * moments.size + 8 * rows * finals
        ),
        name="own",
    )(place, basis_counts, coefs, moments, final_vectors, final_other)

    blocks = []
    for c in range(chunks):
        near, far = halo[c]
        near_other = lax.ppermute(near, "vib", swap)
        far_other = lax.ppermute(far, "vib", swap)
        half = states // cores
        to_other, to_own = pl.pallas_call(
            functools.partial(halo_kernel, places),
            out_shape=[jax.ShapeDtypeStruct((half, width), F32)] * 2,
            grid=(rows // block,),
            in_specs=[
                smem,
                smem,
                smem,
                pl.BlockSpec((1, block, whole), lambda j: (1, j, 0)),
                *[pl.BlockSpec((rows, width), lambda j: (0, 0))] * 4,
                pl.BlockSpec((block, kblocks * width), lambda j: (j, 0)),
                pl.BlockSpec((states, block), lambda j: (0, j)),
                pl.BlockSpec((states, block), lambda j: (0, rows // block + j)),
            ],
            out_specs=[pl.BlockSpec((half, width), lambda j: (0, 0))] * 2,
            scratch_shapes=[
                pltpu.VMEM((whole, kblocks * width), BF16),
                pltpu.VMEM((states, width), F32),
            ],
            cost_estimate=cost(
                2 * rows * whole * kblocks * width + 8 * rows * states * width,
                moments.size + 4 * rows * states,
            ),
            name="halo",
        )(
            place, basis_counts, coefs, moments, near, near_other, far, far_other,
            partial[c], init_t, init_t,
        )
        received = lax.ppermute(to_other, "vib", swap)
        sums = pl.pallas_call(
            add_kernel,
            out_shape=[jax.ShapeDtypeStruct((share, width), F32)] * places,
            in_specs=[vmem] * 2,
            out_specs=[vmem] * places,
            cost_estimate=cost(0, 12 * half * width),
            name="add",
        )(to_own, received)
        blocks.append(sums[0])
        for s in range(1, places):
            turn = [(a, (a + s) % places) for a in range(places)]
            blocks.append(lax.ppermute(sums[s], "ka", turn))

    return pl.pallas_call(
        functools.partial(finish_kernel, places),
        out_shape=jax.ShapeDtypeStruct((share, finals), F32),
        in_specs=[vmem] * len(blocks),
        out_specs=vmem,
        cost_estimate=cost(0, 4 * share * finals * (places + 1)),
        name="finish",
    )(*blocks)


def solution(mesh):
    in_specs = (
        P(None, "vib", None),
        P("ka", "vib", "grp"),
        P("ka", "vib", ("grp", "fin")),
        P(("grp", "ka")),
    )
    out_specs = P(("grp", "ka", "vib"), "fin")
    return jax.shard_map(
        on_device, mesh=mesh, in_specs=in_specs, out_specs=out_specs, check_vma=False
    )
```

```python
import functools

import jax
import jax.numpy as jnp
import numpy as np
from jax import lax
from jax.experimental import pallas as pl
from jax.experimental.pallas import tpu as pltpu
from jax.sharding import PartitionSpec as P


JQ = 30
CHUNKS = 1
BF16, F32 = jnp.bfloat16, jnp.float32


def coefficient_table(positions, kblocks):
    total = positions * kblocks
    jsquare = np.float32(JQ * (JQ + 1))
    norm = np.sqrt(jsquare)
    k = (np.arange(total) - total // 2).astype(np.float32)
    same = k / norm
    upper = np.float32(0.5) * np.sqrt(jsquare - k * (k + np.float32(1.0))) / norm
    lower = np.float32(-0.5) * np.sqrt(jsquare - k * (k - np.float32(1.0))) / norm
    rows = []
    for a in range(positions):
        first, last = a * kblocks, a * kblocks + 1
        before = upper[first - 1] if first > 0 else 0.0
        after = lower[last + 1] if last + 1 < total else 0.0
        rows.append([same[first], same[last], lower[last], upper[first], before, after, 0.0, 0.0])
    return np.asarray(rows, np.float32)


def mask_rows(x, count, start):
    row = lax.broadcasted_iota(jnp.int32, x.shape, 0) + start
    return jnp.where(row < count, x.astype(F32), 0.0).astype(x.dtype)


def own_kernel(chunks, block, table, counts, moments, mine, other, *rest):
    outs, rhs = rest[:chunks], rest[chunks]
    position, core = lax.axis_index("ka"), lax.axis_index("vib")
    kblocks, rows, states = mine.shape
    width = states // chunks
    for half, source in ((core, mine), (1 - core, other)):
        start = pl.multiple_of(half * rows, rows)
        for k in range(kblocks):
            live = mask_rows(source[k], counts[k], start)
            for c in range(chunks):
                at = (c * kblocks + k) * width
                rhs[pl.ds(start, rows), at : at + width] = live[:, c * width : (c + 1) * width]

    for v in range(0, rows, block):
        z = jnp.dot(moments[0, v : v + block, :], rhs[...], preferred_element_type=F32)
        x = jnp.dot(moments[1, v : v + block, :], rhs[...], preferred_element_type=F32)
        for c in range(chunks):
            lo, mid, hi = (2 * c) * width, (2 * c + 1) * width, (2 * c + 2) * width
            low = table[position, 0] * z[:, lo:mid] + table[position, 2] * x[:, mid:hi]
            high = table[position, 1] * z[:, mid:hi] + table[position, 3] * x[:, lo:mid]
            outs[c][v : v + block, :width] = low
            outs[c][v : v + block, width:] = high


def halo_kernel(
    places, block, table, counts, moments, pair_mine, pair_other, next_mine, next_other,
    partial, initial, to_other, to_own, rhs, total,
):
    position, core = lax.axis_index("ka"), lax.axis_index("vib")
    parity = lax.rem(position, 2)
    rows, width = pair_mine.shape
    pair_at = pl.multiple_of((1 - parity) * width, width)
    next_at = pl.multiple_of(parity * width, width)
    mine_at = pl.multiple_of(core * rows, rows)
    other_at = pl.multiple_of((1 - core) * rows, rows)
    rhs[pl.ds(mine_at, rows), pl.ds(pair_at, width)] = pair_mine[...]
    rhs[pl.ds(other_at, rows), pl.ds(pair_at, width)] = pair_other[...]
    rhs[pl.ds(mine_at, rows), pl.ds(next_at, width)] = next_mine[...]
    rhs[pl.ds(other_at, rows), pl.ds(next_at, width)] = next_other[...]

    for v in range(0, rows, block):
        x = jnp.dot(moments[1, v : v + block, :], rhs[...], preferred_element_type=F32)
        row = lax.broadcasted_iota(jnp.int32, (block, width), 0) + core * rows + v
        for k in range(2):
            cols = slice(k * width, (k + 1) * width)
            image = partial[v : v + block, cols] + table[position, 4 + k] * x[:, cols]
            image = jnp.where(row < counts[k], image, 0.0)
            high = image.astype(BF16)
            low = (image - high.astype(F32)).astype(BF16)
            both = lax.dot_general(
                initial[k, v : v + block, :],
                jnp.concatenate([high, low], axis=1),
                (((0,), (0,)), ((), ())),
                preferred_element_type=F32,
            )
            both = both[:, :width] + both[:, width:]
            if v == 0 and k == 0:
                total[...] = both
            else:
                total[...] += both

    share = to_own.shape[0] // places
    for s in range(places):
        dest = lax.rem(position + s, places)
        own_at = pl.multiple_of((dest * 2 + core) * share, share)
        other_at = pl.multiple_of((dest * 2 + 1 - core) * share, share)
        to_own[s * share : (s + 1) * share, :] = total[pl.ds(own_at, share), :]
        to_other[s * share : (s + 1) * share, :] = total[pl.ds(other_at, share), :]


def cost(flops, moved):
    return pl.CostEstimate(flops=int(flops), bytes_accessed=int(moved), transcendentals=0)


def kernel_params(mib):
    return pltpu.CompilerParams(vmem_limit_bytes=mib << 20)


def on_device(moments, initial_vectors, final_vectors, basis_counts):
    kblocks, rows, states = initial_vectors.shape
    finals = final_vectors.shape[2]
    whole = moments.shape[2]
    places, cores = lax.axis_size("ka"), lax.axis_size("vib")
    if kblocks != 2 or cores != 2 or places % 2:
        raise ValueError("unsupported mesh")
    chunks = CHUNKS if finals % (CHUNKS * 128) == 0 else 1
    width = finals // chunks
    share = states // (places * cores)
    half = states // cores
    block = 256

    position, core = lax.axis_index("ka"), lax.axis_index("vib")
    parity = position % 2
    table = jnp.asarray(coefficient_table(places, kblocks))
    swap = [(0, 1), (1, 0)]
    pair = [(a, a + 1 - 2 * (a % 2)) for a in range(places)]
    other_side = [(a, min(max(a - 1 + 2 * (a % 2), 0), places - 1)) for a in range(places)]
    smem = pl.BlockSpec(memory_space=pltpu.SMEM)
    vmem = pl.BlockSpec(memory_space=pltpu.VMEM)

    final_other = lax.ppermute(final_vectors, "vib", swap)

    row = core * rows + lax.broadcasted_iota(jnp.int32, (rows, 1), 0)
    halo = []
    for c in range(chunks):
        sides = []
        for k, targets in ((1 - parity, pair), (parity, other_side)):
            block_of = lax.dynamic_slice(
                final_vectors, (k, 0, c * width), (1, rows, width)
            )[0]
            live = row < lax.dynamic_index_in_dim(basis_counts, k, 0, False)
            payload = jnp.where(live, block_of, jnp.zeros((), BF16))
            sides.append(lax.ppermute(payload, "ka", targets))
        halo.append(sides)

    partial = pl.pallas_call(
        functools.partial(own_kernel, chunks, block),
        out_shape=[jax.ShapeDtypeStruct((rows, kblocks * width), F32)] * chunks,
        in_specs=[smem, smem, vmem, vmem, vmem],
        out_specs=[vmem] * chunks,
        scratch_shapes=[pltpu.VMEM((whole, kblocks * finals), BF16)],
        cost_estimate=cost(
            4 * rows * whole * kblocks * finals, 2 * moments.size + 8 * rows * finals
        ),
        compiler_params=kernel_params(20),
        name="own",
    )(table, basis_counts, moments, final_vectors, final_other)

    blocks = []
    for c in range(chunks):
        near, far = halo[c]
        near_other = lax.ppermute(near, "vib", swap)
        far_other = lax.ppermute(far, "vib", swap)
        to_other, to_own = pl.pallas_call(
            functools.partial(halo_kernel, places, block),
            out_shape=[jax.ShapeDtypeStruct((half, width), F32)] * 2,
            in_specs=[smem, smem] + [vmem] * 7,
            out_specs=[vmem] * 2,
            scratch_shapes=[
                pltpu.VMEM((whole, kblocks * width), BF16),
                pltpu.VMEM((states, width), F32),
            ],
            cost_estimate=cost(
                2 * rows * whole * kblocks * width + 8 * rows * states * width,
                moments.size + 4 * rows * states,
            ),
            compiler_params=kernel_params(20),
            name="halo",
        )(
            table, basis_counts, moments, near, near_other, far, far_other,
            partial[c], initial_vectors,
        )
        received = lax.ppermute(to_other, "vib", swap)
        sums = (to_own + received).reshape(places, share, width)
        terms = [sums[0]]
        for s in range(1, places):
            turn = [(a, (a + s) % places) for a in range(places)]
            terms.append(lax.ppermute(sums[s], "ka", turn))
        blocks.append(terms)

    columns = []
    for terms in blocks:
        amplitude = terms[0]
        for term in terms[1:]:
            amplitude = amplitude + term
        columns.append(amplitude * amplitude)
    return jnp.concatenate(columns, axis=1)


def solution(mesh):
    in_specs = (
        P(None, "vib", None),
        P("ka", "vib", "grp"),
        P("ka", "vib", ("grp", "fin")),
        P(("grp", "ka")),
    )
    out_specs = P(("grp", "ka", "vib"), "fin")

    return jax.shard_map(
        on_device, mesh=mesh, in_specs=in_specs, out_specs=out_specs, check_vma=False
    )
```

```python
import functools

import jax
import jax.numpy as jnp
from jax import lax
from jax.experimental import pallas as pl
from jax.experimental.pallas import tpu as pltpu
from jax.sharding import PartitionSpec as P


JQ = 30
CHUNKS = 1
BF16, F32 = jnp.bfloat16, jnp.float32


def couplings(position, kblocks, width):
    total = lax.axis_size("ka") * kblocks
    jsquare = float(JQ * (JQ + 1))
    norm = jnp.sqrt(jnp.full((1, width), jsquare, F32))

    def k_value(k):
        return jnp.full((1, width), (k - total // 2).astype(F32), F32)

    first = position * kblocks
    rows = []
    for j in range(kblocks):
        k = first + j
        here, under, over = k_value(k), k_value(k - 1), k_value(k + 1)
        upper = 0.5 * jnp.sqrt(jnp.maximum(jsquare - under * (under + 1.0), 0.0)) / norm
        lower = -0.5 * jnp.sqrt(jnp.maximum(jsquare - over * (over - 1.0), 0.0)) / norm
        upper = jnp.where(k > 0, upper, 0.0)
        lower = jnp.where(k < total - 1, lower, 0.0)
        rows.append((here / norm, upper, lower))
    return rows


def keep_rows(x, count, start):
    row = lax.broadcasted_iota(jnp.int32, x.shape, 0) + start
    return jnp.where(row < count, x.astype(F32), 0.0).astype(x.dtype)


def pack_kernel(chunks, counts, final, *rest):
    outs, (held, live, sems) = rest[: 2 * chunks], rest[2 * chunks :]
    position, core = lax.axis_index("ka"), lax.axis_index("vib")
    parity = lax.rem(position, 2)
    rows, states = held.shape[1:]
    width = states // chunks
    sizes = pltpu.make_async_copy(counts, live, sems.at[2])
    sizes.start()
    copies = []
    for slot, k in enumerate((1 - parity, parity)):
        copies.append(pltpu.make_async_copy(final.at[k], held.at[slot], sems.at[slot]))
        copies[-1].start()
    sizes.wait()
    for slot, k in enumerate((1 - parity, parity)):
        copies[slot].wait()
        for c in range(chunks):
            block = held[slot, :, c * width : (c + 1) * width]
            outs[2 * c + slot][...] = keep_rows(block, live[k], core * rows)


def own_kernel(chunks, block, counts, moments, other, *rest):
    payload, outs = rest[: 2 * chunks], rest[2 * chunks : 3 * chunks]
    cross, rhs, direct, live, sems = rest[3 * chunks :]
    position, core = lax.axis_index("ka"), lax.axis_index("vib")
    parity = lax.rem(position, 2)
    kblocks, rows, states = other.shape
    width = states // chunks
    steps = rows // block
    sizes = pltpu.make_async_copy(counts, live, sems.at[2 * steps])
    sizes.start()
    copies = []
    for s in range(steps):
        at = pl.ds(s * block, block)
        for m, target in ((0, direct), (1, cross)):
            copies.append(
                pltpu.make_async_copy(moments.at[m, at], target.at[at], sems.at[2 * s + m])
            )
            copies[-1].start()
    mine_at = pl.multiple_of(core * rows, rows)
    other_at = pl.multiple_of((1 - core) * rows, rows)
    for c in range(chunks):
        for slot, k in enumerate((1 - parity, parity)):
            at = pl.multiple_of((c * kblocks + k) * width, width)
            rhs[pl.ds(mine_at, rows), pl.ds(at, width)] = payload[2 * c + slot][...]
    sizes.wait()
    for k in range(kblocks):
        block_of = keep_rows(other[k], live[k], other_at)
        for c in range(chunks):
            at = (c * kblocks + k) * width
            rhs[pl.ds(other_at, rows), at : at + width] = block_of[:, c * width : (c + 1) * width]

    (same_low, _, lower), (same_high, upper, _) = couplings(position, kblocks, width)
    for s in range(steps):
        v = slice(s * block, (s + 1) * block)
        copies[2 * s].wait()
        z = jnp.dot(direct[v, :], rhs[...], preferred_element_type=F32)
        copies[2 * s + 1].wait()
        x = jnp.dot(cross[v, :], rhs[...], preferred_element_type=F32)
        for c in range(chunks):
            lo, mid, hi = (2 * c) * width, (2 * c + 1) * width, (2 * c + 2) * width
            outs[c][v, :width] = same_low * z[:, lo:mid] + lower * x[:, mid:hi]
            outs[c][v, width:] = same_high * z[:, mid:hi] + upper * x[:, lo:mid]


def halo_kernel(
    places, block, counts, cross, pair_mine, pair_other, next_mine, next_other,
    partial, initial, to_other, to_own, rhs, images, total, live, sems,
):
    sizes = pltpu.make_async_copy(counts, live, sems.at[0])
    sizes.start()
    position, core = lax.axis_index("ka"), lax.axis_index("vib")
    parity = lax.rem(position, 2)
    rows, width = pair_mine.shape
    states = initial.shape[2]
    pair_at = pl.multiple_of((1 - parity) * width, width)
    next_at = pl.multiple_of(parity * width, width)
    mine_at = pl.multiple_of(core * rows, rows)
    other_at = pl.multiple_of((1 - core) * rows, rows)
    rhs[pl.ds(mine_at, rows), pl.ds(pair_at, width)] = pair_mine[...]
    rhs[pl.ds(other_at, rows), pl.ds(pair_at, width)] = pair_other[...]
    rhs[pl.ds(mine_at, rows), pl.ds(next_at, width)] = next_mine[...]
    rhs[pl.ds(other_at, rows), pl.ds(next_at, width)] = next_other[...]
    (_, upper, _), (_, _, lower) = couplings(position, 2, width)
    sizes.wait()

    for v in range(0, rows, block):
        x = jnp.dot(cross[v : v + block, :], rhs[...], preferred_element_type=F32)
        row = lax.broadcasted_iota(jnp.int32, (block, width), 0) + core * rows + v
        for k, weight in ((0, upper), (1, lower)):
            cols = slice(k * width, (k + 1) * width)
            image = partial[v : v + block, cols] + weight * x[:, cols]
            image = jnp.where(row < live[k], image, 0.0)
            high = image.astype(BF16)
            images[k * rows + v : k * rows + v + block, :width] = high
            images[k * rows + v : k * rows + v + block, width:] = (
                image - high.astype(F32)
            ).astype(BF16)

    vectors = initial.reshape(2 * rows, states)
    for i in range(0, states, block):
        both = lax.dot_general(
            vectors[:, i : i + block],
            images[...],
            (((0,), (0,)), ((), ())),
            preferred_element_type=F32,
        )
        total[i : i + block, :] = both[:, :width] + both[:, width:]

    share = to_own.shape[0] // places
    for s in range(places):
        dest = lax.rem(position + s, places)
        own_at = pl.multiple_of((dest * 2 + core) * share, share)
        other_at = pl.multiple_of((dest * 2 + 1 - core) * share, share)
        to_own[s * share : (s + 1) * share, :] = total[pl.ds(own_at, share), :]
        to_other[s * share : (s + 1) * share, :] = total[pl.ds(other_at, share), :]


def cost(flops, moved):
    return pl.CostEstimate(flops=int(flops), bytes_accessed=int(moved), transcendentals=0)


def kernel_params(mib):
    return pltpu.CompilerParams(vmem_limit_bytes=mib << 20)


def on_device(moments, initial_vectors, final_vectors, basis_counts):
    kblocks, rows, states = initial_vectors.shape
    finals = final_vectors.shape[2]
    whole = moments.shape[2]
    places, cores = lax.axis_size("ka"), lax.axis_size("vib")
    if kblocks != 2 or cores != 2 or places % 2:
        raise ValueError("unsupported mesh")
    chunks = CHUNKS if finals % (CHUNKS * 128) == 0 else 1
    width = finals // chunks
    share = states // (places * cores)
    half = states // cores
    block = 256

    def resting(x):
        return pltpu.with_memory_space_constraint(x, pltpu.HBM)

    swap = [(0, 1), (1, 0)]
    pair = [(a, a + 1 - 2 * (a % 2)) for a in range(places)]
    other_side = [(a, min(max(a - 1 + 2 * (a % 2), 0), places - 1)) for a in range(places)]
    vmem = pl.BlockSpec(memory_space=pltpu.VMEM)
    hbm = pl.BlockSpec(memory_space=pltpu.HBM)
    counted = pltpu.SMEM((kblocks,), jnp.int32)

    payload = pl.pallas_call(
        functools.partial(pack_kernel, chunks),
        out_shape=[jax.ShapeDtypeStruct((rows, width), BF16)] * (2 * chunks),
        in_specs=[hbm, hbm],
        out_specs=[vmem] * (2 * chunks),
        scratch_shapes=[
            pltpu.VMEM((kblocks, rows, finals), BF16),
            counted,
            pltpu.SemaphoreType.DMA((3,)),
        ],
        cost_estimate=cost(0, 4 * kblocks * rows * finals),
        compiler_params=kernel_params(8),
        name="pack",
    )(resting(basis_counts), resting(final_vectors))

    halo = []
    for c in range(chunks):
        near = lax.ppermute(payload[2 * c], "ka", pair)
        far = lax.ppermute(payload[2 * c + 1], "ka", other_side)
        halo.append((near, far))
    final_other = lax.ppermute(final_vectors, "vib", swap)

    *partial, cross = pl.pallas_call(
        functools.partial(own_kernel, chunks, block),
        out_shape=[jax.ShapeDtypeStruct((rows, kblocks * width), F32)] * chunks
        + [jax.ShapeDtypeStruct((rows, whole), BF16)],
        in_specs=[hbm, hbm] + [vmem] * (1 + 2 * chunks),
        out_specs=[vmem] * (chunks + 1),
        scratch_shapes=[
            pltpu.VMEM((whole, kblocks * finals), BF16),
            pltpu.VMEM((rows, whole), BF16),
            counted,
            pltpu.SemaphoreType.DMA((2 * (rows // block) + 1,)),
        ],
        cost_estimate=cost(
            4 * rows * whole * kblocks * finals, 2 * moments.size + 8 * rows * finals
        ),
        compiler_params=kernel_params(20),
        name="own",
    )(resting(basis_counts), resting(moments), final_other, *payload)

    blocks = []
    for c in range(chunks):
        near, far = halo[c]
        near_other = lax.ppermute(near, "vib", swap)
        far_other = lax.ppermute(far, "vib", swap)
        to_other, to_own = pl.pallas_call(
            functools.partial(halo_kernel, places, block),
            out_shape=[jax.ShapeDtypeStruct((half, width), F32)] * 2,
            in_specs=[hbm] + [vmem] * 7,
            out_specs=[vmem] * 2,
            scratch_shapes=[
                pltpu.VMEM((whole, kblocks * width), BF16),
                pltpu.VMEM((kblocks * rows, 2 * width), BF16),
                pltpu.VMEM((states, width), F32),
                counted,
                pltpu.SemaphoreType.DMA((1,)),
            ],
            cost_estimate=cost(
                2 * rows * whole * kblocks * width + 8 * rows * states * width,
                moments.size + 4 * rows * states,
            ),
            compiler_params=kernel_params(20),
            name="halo",
        )(
            resting(basis_counts), cross, near, near_other, far, far_other, partial[c],
            initial_vectors,
        )
        received = lax.ppermute(to_other, "vib", swap)
        sums = (to_own + received).reshape(places, share, width)
        terms = [sums[0]]
        for s in range(1, places):
            turn = [(a, (a + s) % places) for a in range(places)]
            terms.append(lax.ppermute(sums[s], "ka", turn))
        blocks.append(terms)

    columns = []
    for terms in blocks:
        amplitude = terms[0]
        for term in terms[1:]:
            amplitude = amplitude + term
        columns.append(amplitude * amplitude)
    return jnp.concatenate(columns, axis=1)


def solution(mesh):
    in_specs = (
        P(None, "vib", None),
        P("ka", "vib", "grp"),
        P("ka", "vib", ("grp", "fin")),
        P(("grp", "ka")),
    )
    out_specs = P(("grp", "ka", "vib"), "fin")

    return jax.shard_map(
        on_device, mesh=mesh, in_specs=in_specs, out_specs=out_specs, check_vma=False
    )
```

```python
import functools

import jax
import jax.numpy as jnp
from jax import lax
from jax.experimental import pallas as pl
from jax.experimental.pallas import tpu as pltpu
from jax.sharding import PartitionSpec as P


JQ = 30
BF16, F32 = jnp.bfloat16, jnp.float32
TINY = 1e-30
SCALE_ROWS = 16


def couplings(position, kblocks, width):
    total = lax.axis_size("ka") * kblocks
    jsquare = float(JQ * (JQ + 1))
    norm = jnp.sqrt(jnp.full((1, width), jsquare, F32))

    def k_value(k):
        return jnp.full((1, width), (k - total // 2).astype(F32), F32)

    first = position * kblocks
    rows = []
    for j in range(kblocks):
        k = first + j
        here, under, over = k_value(k), k_value(k - 1), k_value(k + 1)
        upper = 0.5 * jnp.sqrt(jnp.maximum(jsquare - under * (under + 1.0), 0.0)) / norm
        lower = -0.5 * jnp.sqrt(jnp.maximum(jsquare - over * (over - 1.0), 0.0)) / norm
        upper = jnp.where(k > 0, upper, 0.0)
        lower = jnp.where(k < total - 1, lower, 0.0)
        rows.append((here / norm, upper, lower))
    return rows


def keep_rows(x, count, start):
    row = lax.broadcasted_iota(jnp.int32, x.shape, 0) + start
    return jnp.where(row < count, x.astype(F32), 0.0).astype(x.dtype)


def pack_kernel(counts, final, near, far, held, live, sems):
    position, core = lax.axis_index("ka"), lax.axis_index("vib")
    parity = lax.rem(position, 2)
    rows = near.shape[0]
    sizes = pltpu.make_async_copy(counts, live, sems.at[2])
    sizes.start()
    copies = []
    for slot, k in enumerate((1 - parity, parity)):
        copies.append(pltpu.make_async_copy(final.at[k], held.at[slot], sems.at[slot]))
        copies[-1].start()
    sizes.wait()
    for slot, (k, out) in enumerate(((1 - parity, near), (parity, far))):
        copies[slot].wait()
        out[...] = keep_rows(held[slot], live[k], core * rows)


def own_kernel(block, counts, moments, other, near, far, out, rhs, live, sems):
    position, core = lax.axis_index("ka"), lax.axis_index("vib")
    parity = lax.rem(position, 2)
    kblocks, rows, width = other.shape
    sizes = pltpu.make_async_copy(counts, live, sems.at[0])
    sizes.start()
    mine_at = pl.multiple_of(core * rows, rows)
    other_at = pl.multiple_of((1 - core) * rows, rows)
    for k, source in ((1 - parity, near), (parity, far)):
        at = pl.multiple_of(k * width, width)
        rhs[pl.ds(mine_at, rows), pl.ds(at, width)] = source[...]
    sizes.wait()
    for k in range(kblocks):
        rhs[pl.ds(other_at, rows), k * width : (k + 1) * width] = keep_rows(
            other[k], live[k], other_at
        )

    (same_low, _, lower), (same_high, upper, _) = couplings(position, kblocks, width)
    for start in range(0, rows, block):
        v = slice(start, start + block)
        z = jnp.dot(moments[0, v, :], rhs[...], preferred_element_type=F32)
        x = jnp.dot(moments[1, v, :], rhs[...], preferred_element_type=F32)
        out[v, :width] = same_low * z[:, :width] + lower * x[:, width:]
        out[v, width:] = same_high * z[:, width:] + upper * x[:, :width]


def side_kernel(places, block, is_near, counts, moments, mine, other, partial, initial, *rest):
    if is_near:
        total, images, live, sems = rest
    else:
        before, to_other, to_own, images, total, live, sems = rest
    sizes = pltpu.make_async_copy(counts, live, sems.at[0])
    sizes.start()
    position, core = lax.axis_index("ka"), lax.axis_index("vib")
    parity = lax.rem(position, 2)
    k = 1 - parity if is_near else parity
    rows, width = mine.shape
    states = initial.shape[2]
    mine_at = pl.multiple_of(core * rows, rows)
    other_at = pl.multiple_of((1 - core) * rows, rows)
    columns = pl.ds(pl.multiple_of(k * width, width), width)
    (_, upper, _), (_, _, lower) = couplings(position, 2, width)
    weight = jnp.where(k == 0, upper, lower)
    sizes.wait()

    for v in range(0, rows, block):
        at = slice(v, v + block)
        x = jnp.dot(
            moments[1, at, pl.ds(mine_at, rows)], mine[...], preferred_element_type=F32
        ) + jnp.dot(
            moments[1, at, pl.ds(other_at, rows)], other[...], preferred_element_type=F32
        )
        row = lax.broadcasted_iota(jnp.int32, (block, width), 0) + core * rows + v
        image = partial[at, columns] + weight * x
        image = jnp.where(row < live[k], image, 0.0)
        high = image.astype(BF16)
        images[at, :width] = high
        images[at, width:] = (image - high.astype(F32)).astype(BF16)

    for i in range(0, states, block):
        both = lax.dot_general(
            initial[k, :, i : i + block],
            images[...],
            (((0,), (0,)), ((), ())),
            preferred_element_type=F32,
        )
        both = both[:, :width] + both[:, width:]
        total[i : i + block, :] = both if is_near else both + before[i : i + block, :]

    if is_near:
        return
    share = to_own.shape[0] // places
    for s in range(places):
        dest = lax.rem(position + s, places)
        own_at = pl.multiple_of((dest * 2 + core) * share, share)
        other_at = pl.multiple_of((dest * 2 + 1 - core) * share, share)
        to_own[s * share : (s + 1) * share, :] = total[pl.ds(own_at, share), :]
        to_other[s * share : (s + 1) * share, :] = total[pl.ds(other_at, share), :]


def code_kernel(mine, other, own, *outs):
    share, width = own.shape
    own[...] = mine[:share, :] + other[:share, :]
    for s, out in enumerate(outs, 1):
        rows = slice(s * share, (s + 1) * share)
        value = mine[rows, :] + other[rows, :]
        peak = jnp.maximum(jnp.max(jnp.abs(value), axis=0, keepdims=True), TINY)
        exponent = jnp.floor(jnp.log2(peak)) + 1.0
        code = jnp.floor(value * jnp.exp2(15.0 - exponent) + 0.5)
        code = jnp.clip(code, -32767.0, 32767.0)
        out[:share, :] = code.astype(jnp.int32).astype(jnp.int16)
        spread = jnp.broadcast_to(exponent, (out.shape[0] - share, width))
        out[share:, :] = spread.astype(jnp.int32).astype(jnp.int16)


def decode(coded, share):
    exponent = coded[share : share + 1].astype(F32)
    return coded[:share].astype(F32) * jnp.exp2(exponent - 15.0)


def cost(flops, moved):
    return pl.CostEstimate(flops=int(flops), bytes_accessed=int(moved), transcendentals=0)


def kernel_params(mib):
    return pltpu.CompilerParams(vmem_limit_bytes=mib << 20)


def on_device(moments, initial_vectors, final_vectors, basis_counts):
    kblocks, rows, states = initial_vectors.shape
    width = final_vectors.shape[2]
    whole = moments.shape[2]
    places, cores = lax.axis_size("ka"), lax.axis_size("vib")
    if kblocks != 2 or cores != 2 or places % 2:
        raise ValueError("unsupported mesh")
    share = states // (places * cores)
    half = states // cores
    block = 256

    def resting(x):
        return pltpu.with_memory_space_constraint(x, pltpu.HBM)

    swap = [(0, 1), (1, 0)]
    pair = [(a, a + 1 - 2 * (a % 2)) for a in range(places)]
    other_side = [(a, min(max(a - 1 + 2 * (a % 2), 0), places - 1)) for a in range(places)]
    vmem = pl.BlockSpec(memory_space=pltpu.VMEM)
    hbm = pl.BlockSpec(memory_space=pltpu.HBM)
    counted = pltpu.SMEM((kblocks,), jnp.int32)
    counts = resting(basis_counts)

    near_out, far_out = pl.pallas_call(
        pack_kernel,
        out_shape=[jax.ShapeDtypeStruct((rows, width), BF16)] * 2,
        in_specs=[hbm, hbm],
        out_specs=[vmem] * 2,
        scratch_shapes=[
            pltpu.VMEM((kblocks, rows, width), BF16),
            counted,
            pltpu.SemaphoreType.DMA((3,)),
        ],
        cost_estimate=cost(8 * rows * whole * width, 4 * kblocks * rows * width),
        compiler_params=kernel_params(8),
        name="pack",
    )(counts, resting(final_vectors))

    near = lax.ppermute(near_out, "ka", pair)
    far = lax.ppermute(far_out, "ka", other_side)
    final_other = lax.ppermute(final_vectors, "vib", swap)

    partial = pl.pallas_call(
        functools.partial(own_kernel, block),
        out_shape=jax.ShapeDtypeStruct((rows, kblocks * width), F32),
        in_specs=[hbm] + [vmem] * 4,
        out_specs=vmem,
        scratch_shapes=[
            pltpu.VMEM((whole, kblocks * width), BF16),
            counted,
            pltpu.SemaphoreType.DMA((1,)),
        ],
        cost_estimate=cost(4 * rows * whole * kblocks * width, 8 * rows * width),
        compiler_params=kernel_params(20),
        name="own",
    )(counts, moments, final_other, near_out, far_out)

    def side(is_near, mine, other, *before):
        outs = [jax.ShapeDtypeStruct((states, width), F32)]
        scratch = [
            pltpu.VMEM((rows, 2 * width), BF16),
            counted,
            pltpu.SemaphoreType.DMA((1,)),
        ]
        if not is_near:
            outs = [jax.ShapeDtypeStruct((half, width), F32)] * 2
            scratch.insert(1, pltpu.VMEM((states, width), F32))
        return pl.pallas_call(
            functools.partial(side_kernel, places, block, is_near),
            out_shape=outs,
            in_specs=[hbm] + [vmem] * (5 + len(before)),
            out_specs=[vmem] * len(outs),
            scratch_shapes=scratch,
            cost_estimate=cost(
                2 * rows * whole * width + 4 * rows * states * width, 4 * rows * states
            ),
            compiler_params=kernel_params(20),
            name="side",
        )(counts, moments, mine, other, partial, initial_vectors, *before)

    near_other = lax.ppermute(near, "vib", swap)
    (before,) = side(True, near, near_other)
    far_other = lax.ppermute(far, "vib", swap)
    to_other, to_own = side(False, far, far_other, before)

    received = lax.ppermute(to_other, "vib", swap)
    amplitude, *coded = pl.pallas_call(
        code_kernel,
        out_shape=[jax.ShapeDtypeStruct((share, width), F32)]
        + [jax.ShapeDtypeStruct((share + SCALE_ROWS, width), jnp.int16)] * (places - 1),
        in_specs=[vmem] * 2,
        out_specs=[vmem] * places,
        cost_estimate=cost(16 * half * width, 12 * half * width),
        compiler_params=kernel_params(8),
        name="code",
    )(to_own, received)
    for s in range(1, places):
        turn = [(a, (a + s) % places) for a in range(places)]
        arrived = lax.ppermute(coded[s - 1], "ka", turn)
        amplitude = amplitude + decode(arrived, share)
    return amplitude * amplitude


def solution(mesh):
    in_specs = (
        P(None, "vib", None),
        P("ka", "vib", "grp"),
        P("ka", "vib", ("grp", "fin")),
        P(("grp", "ka")),
    )
    out_specs = P(("grp", "ka", "vib"), "fin")

    return jax.shard_map(
        on_device, mesh=mesh, in_specs=in_specs, out_specs=out_specs, check_vma=False
    )
```

```python
import functools

import jax
import jax.numpy as jnp
from jax import lax
from jax.experimental import pallas as pl
from jax.experimental.pallas import tpu as pltpu
from jax.sharding import PartitionSpec as P


JQ = 30
BF16, F32 = jnp.bfloat16, jnp.float32
TINY = 1e-30
SCALE_ROWS = 8


def couplings(position, kblocks, width):
    total = lax.axis_size("ka") * kblocks
    jsquare = float(JQ * (JQ + 1))
    norm = jnp.sqrt(jnp.full((1, width), jsquare, F32))

    def k_value(k):
        return jnp.full((1, width), (k - total // 2).astype(F32), F32)

    first = position * kblocks
    rows = []
    for j in range(kblocks):
        k = first + j
        here, under, over = k_value(k), k_value(k - 1), k_value(k + 1)
        upper = 0.5 * jnp.sqrt(jnp.maximum(jsquare - under * (under + 1.0), 0.0)) / norm
        lower = -0.5 * jnp.sqrt(jnp.maximum(jsquare - over * (over - 1.0), 0.0)) / norm
        upper = jnp.where(k > 0, upper, 0.0)
        lower = jnp.where(k < total - 1, lower, 0.0)
        rows.append((here / norm, upper, lower))
    return rows


def keep_rows(x, count, start):
    row = lax.broadcasted_iota(jnp.int32, x.shape, 0) + start
    return jnp.where(row < count, x.astype(F32), 0.0).astype(x.dtype)


def row_limit(limits, k, width):
    return jnp.concatenate([limits[k, :1, :]] * (width // limits.shape[2]), axis=1)


def side_block(is_near):
    parity = lax.rem(lax.axis_index("ka"), 2)
    return 1 - parity if is_near else parity


def pack_kernel(counts, final, near, far, limits, held, live, sems):
    sizes = pltpu.make_async_copy(counts, live, sems.at[2])
    sizes.start()
    sides = ((side_block(False), far), (side_block(True), near))
    copies = []
    for slot, (k, _) in enumerate(sides):
        copies.append(pltpu.make_async_copy(final.at[k], held.at[slot], sems.at[slot]))
        copies[-1].start()
    sizes.wait()
    for k in range(limits.shape[0]):
        limits[k] = jnp.full(limits.shape[1:], live[k], jnp.int32)
    for slot, (k, out) in enumerate(sides):
        copies[slot].wait()
        out[...] = keep_rows(held[slot], live[k], lax.axis_index("vib") * out.shape[0])


def own_kernel(block, limits, moments, other, near, far, out, rhs):
    position, core = lax.axis_index("ka"), lax.axis_index("vib")
    parity = lax.rem(position, 2)
    kblocks, rows, width = other.shape
    mine_at = pl.multiple_of(core * rows, rows)
    other_at = pl.multiple_of((1 - core) * rows, rows)
    for k, source in ((1 - parity, near), (parity, far)):
        at = pl.multiple_of(k * width, width)
        rhs[pl.ds(mine_at, rows), pl.ds(at, width)] = source[...]
    for k in range(kblocks):
        rhs[pl.ds(other_at, rows), k * width : (k + 1) * width] = keep_rows(
            other[k], row_limit(limits, k, width), other_at
        )

    (same_low, _, lower), (same_high, upper, _) = couplings(position, kblocks, width)
    for start in range(0, rows, block):
        v = slice(start, start + block)
        z = jnp.dot(moments[0, v, :], rhs[...], preferred_element_type=F32)
        x = jnp.dot(moments[1, v, :], rhs[...], preferred_element_type=F32)
        out[v, :width] = same_low * z[:, :width] + lower * x[:, width:]
        out[v, width:] = same_high * z[:, width:] + upper * x[:, :width]


def image_kernel(block, is_near, is_mine, limits, moments, piece, base, out):
    position, core = lax.axis_index("ka"), lax.axis_index("vib")
    k = side_block(is_near)
    rows, width = piece.shape
    half_at = pl.multiple_of((core if is_mine else 1 - core) * rows, rows)
    (_, upper, _), (_, _, lower) = couplings(position, 2, width)
    weight = jnp.where(k == 0, upper, lower)
    columns = pl.ds(pl.multiple_of(k * width, width), width) if is_mine else slice(None)
    limit = row_limit(limits, k, width)
    for v in range(0, rows, block):
        at = slice(v, v + block)
        x = jnp.dot(moments[1, at, pl.ds(half_at, rows)], piece[...], preferred_element_type=F32)
        image = base[at, columns] + weight * x
        if is_mine:
            out[at, :] = image
            continue
        row = lax.broadcasted_iota(jnp.int32, (block, width), 0) + core * rows + v
        image = jnp.where(row < limit, image, 0.0)
        high = image.astype(BF16)
        out[at, :width] = high
        out[at, width:] = (image - high.astype(F32)).astype(BF16)


def product_kernel(places, block, is_near, halves, initial, images, *rest):
    outs, before = rest[-len(halves) :], rest[: -len(halves)]
    position, core = lax.axis_index("ka"), lax.axis_index("vib")
    k = side_block(is_near)
    width = images.shape[1] // 2
    share = outs[0].shape[0] // places
    per = max(1, block // share)
    for h, half in enumerate(halves):
        to_core = core if half == "own" else 1 - core
        offsets = [
            pl.multiple_of((lax.rem(position + s, places) * 2 + to_core) * share, share)
            for s in range(places)
        ]
        for s in range(0, places, per):
            vectors = [initial[k, :, pl.ds(o, share)] for o in offsets[s : s + per]]
            both = lax.dot_general(
                jnp.concatenate(vectors, axis=1),
                images[...],
                (((0,), (0,)), ((), ())),
                preferred_element_type=F32,
            )
            both = both[:, :width] + both[:, width:]
            at = slice(s * share, (s + len(vectors)) * share)
            outs[h][at, :] = both + before[h][at, :] if before else both


def narrow_product_kernel(places, block, is_near, initial, images, *rest):
    to_other, to_own, total = rest[-3:]
    before = rest[:-3]
    position, core = lax.axis_index("ka"), lax.axis_index("vib")
    k = side_block(is_near)
    width = images.shape[1] // 2
    share = to_own.shape[0] // places
    for i in range(0, initial.shape[2], block):
        both = lax.dot_general(
            initial[k, :, i : i + block],
            images[...],
            (((0,), (0,)), ((), ())),
            preferred_element_type=F32,
        )
        total[i : i + block, :] = both[:, :width] + both[:, width:]
    for h, (out, to_core) in enumerate(((to_other, 1 - core), (to_own, core))):
        for s in range(places):
            at = slice(s * share, (s + 1) * share)
            start = (lax.rem(position + s, places) * 2 + to_core) * share
            value = total[pl.ds(pl.multiple_of(start, share), share), :]
            out[at, :] = value + before[h][at, :] if before else value


def code_kernel(mine, other, own, *outs):
    share, width = own.shape
    own[...] = mine[:share, :] + other[:share, :]
    for s, out in enumerate(outs, 1):
        rows = slice(s * share, (s + 1) * share)
        value = mine[rows, :] + other[rows, :]
        peak = jnp.maximum(jnp.max(jnp.abs(value), axis=0, keepdims=True), TINY)
        exponent = jnp.floor(jnp.log2(peak)) + 1.0
        code = jnp.floor(value * jnp.exp2(15.0 - exponent) + 0.5)
        code = jnp.clip(code, -32767.0, 32767.0)
        out[:share, :] = code.astype(jnp.int32).astype(jnp.int16)
        spread = jnp.broadcast_to(exponent, (out.shape[0] - share, width))
        out[share:, :] = spread.astype(jnp.int32).astype(jnp.int16)


def decode(coded, share):
    exponent = coded[share : share + 1].astype(F32)
    return coded[:share].astype(F32) * jnp.exp2(exponent - 15.0)


def cost(flops, moved):
    return pl.CostEstimate(flops=int(flops), bytes_accessed=int(moved), transcendentals=0)


def kernel_params(mib):
    return pltpu.CompilerParams(vmem_limit_bytes=mib << 20)


def on_device(moments, initial_vectors, final_vectors, basis_counts):
    kblocks, rows, states = initial_vectors.shape
    width = final_vectors.shape[2]
    whole = moments.shape[2]
    places, cores = lax.axis_size("ka"), lax.axis_size("vib")
    if kblocks != 2 or cores != 2 or places % 2:
        raise ValueError("unsupported mesh")
    share = states // (places * cores)
    half = states // cores
    block = 256

    def resting(x):
        return pltpu.with_memory_space_constraint(x, pltpu.HBM)

    swap = [(0, 1), (1, 0)]
    pair = [(a, a + 1 - 2 * (a % 2)) for a in range(places)]
    fins = lax.axis_size("fin")
    other_side = []
    for a in range(places):
        to = a - 1 + 2 * (a % 2)
        for x in range(fins):
            inside = 0 <= to < places
            other_side.append((a * fins + x, to * fins + x if inside else a * fins + (x ^ 1) % fins))
    vmem = pl.BlockSpec(memory_space=pltpu.VMEM)
    hbm = pl.BlockSpec(memory_space=pltpu.HBM)

    near_out, far_out, limits = pl.pallas_call(
        pack_kernel,
        out_shape=[jax.ShapeDtypeStruct((rows, width), BF16)] * 2
        + [jax.ShapeDtypeStruct((kblocks, 8, 128), jnp.int32)],
        in_specs=[hbm, hbm],
        out_specs=[vmem] * 3,
        scratch_shapes=[
            pltpu.VMEM((kblocks, rows, width), BF16),
            pltpu.SMEM((kblocks,), jnp.int32),
            pltpu.SemaphoreType.DMA((3,)),
        ],
        cost_estimate=cost(8 * rows * whole * width, 4 * kblocks * rows * width),
        compiler_params=kernel_params(8),
        name="pack",
    )(resting(basis_counts), resting(final_vectors))

    far = lax.ppermute(far_out, ("ka", "fin"), other_side)
    near = lax.ppermute(near_out, "ka", pair)
    final_other = lax.ppermute(final_vectors, "vib", swap)

    partial = pl.pallas_call(
        functools.partial(own_kernel, block),
        out_shape=jax.ShapeDtypeStruct((rows, kblocks * width), F32),
        in_specs=[vmem] * 5,
        out_specs=vmem,
        scratch_shapes=[pltpu.VMEM((whole, kblocks * width), BF16)],
        cost_estimate=cost(4 * rows * whole * kblocks * width, 8 * rows * width),
        compiler_params=kernel_params(20),
        name="own",
    )(limits, moments, final_other, near_out, far_out)

    def images(is_near, is_mine, piece, base):
        shape = jax.ShapeDtypeStruct((rows, width), F32)
        if not is_mine:
            shape = jax.ShapeDtypeStruct((rows, 2 * width), BF16)
        return pl.pallas_call(
            functools.partial(image_kernel, block, is_near, is_mine),
            out_shape=shape,
            in_specs=[vmem] * 4,
            out_specs=vmem,
            cost_estimate=cost(2 * rows * rows * width, 16 * rows * width),
            compiler_params=kernel_params(20),
            name="images",
        )(limits, moments, piece, base)

    def product(is_near, halves, pairs_of, *before):
        wide = share % 128 == 0
        kernel = functools.partial(product_kernel, places, block, is_near, halves)
        if not wide:
            kernel = functools.partial(narrow_product_kernel, places, block, is_near)
        return pl.pallas_call(
            kernel,
            out_shape=[jax.ShapeDtypeStruct((half, width), F32)] * len(halves),
            in_specs=[vmem] * (2 + len(before)),
            out_specs=[vmem] * len(halves),
            scratch_shapes=[] if wide else [pltpu.VMEM((states, width), F32)],
            cost_estimate=cost(4 * rows * half * len(halves) * width, 8 * rows * width),
            compiler_params=kernel_params(20),
            name="product",
        )(initial_vectors, pairs_of, *before)

    far_other = lax.ppermute(far, "vib", swap)
    far_base = images(False, True, far, partial)
    far_images = images(False, False, far_other, far_base)
    near_other = lax.ppermute(near, "vib", swap)
    before = product(False, ("other", "own"), far_images)
    near_base = images(True, True, near, partial)
    near_images = images(True, False, near_other, near_base)
    if share % 128 == 0:
        (to_other,) = product(True, ("other",), near_images, before[0])
    else:
        to_other, to_own = product(True, ("other", "own"), near_images, *before)
    received = lax.ppermute(to_other, "vib", swap)
    if share % 128 == 0:
        (to_own,) = product(True, ("own",), near_images, before[1])
    amplitude, *coded = pl.pallas_call(
        code_kernel,
        out_shape=[jax.ShapeDtypeStruct((share, width), F32)]
        + [jax.ShapeDtypeStruct((share + SCALE_ROWS, width), jnp.int16)] * (places - 1),
        in_specs=[vmem] * 2,
        out_specs=[vmem] * places,
        cost_estimate=cost(16 * half * width, 12 * half * width),
        compiler_params=kernel_params(8),
        name="code",
    )(to_own, received)
    for s in range(1, places):
        turn = [(a, (a + s) % places) for a in range(places)]
        arrived = lax.ppermute(coded[s - 1], "ka", turn)
        amplitude = amplitude + decode(arrived, share)
    return amplitude * amplitude


def solution(mesh):
    in_specs = (
        P(None, "vib", None),
        P("ka", "vib", "grp"),
        P("ka", "vib", ("grp", "fin")),
        P(("grp", "ka")),
    )
    out_specs = P(("grp", "ka", "vib"), "fin")

    return jax.shard_map(
        on_device, mesh=mesh, in_specs=in_specs, out_specs=out_specs, check_vma=False
    )
```
